32 devices in a mesh: bulk: 4 (over y, x), cuts: 8 (over z, core).
Axes of the slice: x: 2, y: 2, z: 4, core: 2. Of those that a mesh axis runs over, the one named last changes fastest.
Arguments:
- amplitudes: bfloat16 [16384, 8192], P('bulk', 'cuts'), may hold values from -6 to 6
- amp_tiles: int32 [128, 64], P('bulk', 'cuts'), may hold values from 0 to 1, as said below
- occ_coupling: bfloat16 [128, 128], replicated, may hold values from -0.5 to 0.5
- integrals: bfloat16 [8192, 2048], P('cuts'), may hold values from -0.09375 to 0.09375
- int_tiles: int32 [64, 16], P('cuts'), may hold values from 0 to 1, as said below
Outputs:
- residual: bfloat16 [2048, 16384], P('cuts', 'bulk')
The draws below stay inside these ranges and needn't reach their ends.
Inputs may be any that keep to these rules, and one draw needn't show every extreme that they name: `amp_tiles`: 1 where a tile is kept; kept tiles follow the distance, round a cycle of fragments, between the fragments of the two tile indices: each row of tiles keeps a band of columns near its own fragment and one near the fragment opposite on the cycle, whose width varies from group to group of rows. `int_tiles`: 1 where a tile is kept; kept tiles follow the distance, round a cycle of fragments, between the fragments of the two tile indices: each row of tiles keeps a band of columns near its own fragment and one near the fragment opposite on the cycle, whose width varies from group to group of rows.
All inputs are finite; a program needn't handle non-finite values.
Results may differ from the reference program's by a relative error of at most 0.0095.
Values may be sent and summed in bfloat16 or wider, within the bound.
A program may use at most 128 MiB of HBM per device.

```python
import jax
import jax.numpy as jnp
from jax import lax

TILE = 128
OCC = 128
CD_DEV = 1024
NO = 16384
NV = 8192
NA = 2048
N_CUTS = 8


def locality(key, rows, cols, salt):
    first, second, third = jax.random.split(jax.random.fold_in(key, salt), 3)
    row_pos = jnp.arange(rows, dtype=jnp.int32) * 64 // rows + jax.random.randint(first, (rows,), -2, 3)
    col_pos = jnp.arange(cols, dtype=jnp.int32) * 64 // cols + jax.random.randint(second, (cols,), -2, 3)
    group = jnp.arange(rows, dtype=jnp.int32) * 16 // rows
    widths = jax.random.randint(third, (16,), 1, 12)[group]
    apart = jnp.mod(row_pos[:, None] - col_pos[None, :] + 128, 64)
    circle = jnp.minimum(apart, 64 - apart)
    near = circle <= widths[:, None]
    across = jnp.abs(circle - 32) <= widths[:, None]
    return jnp.logical_or(near, across).astype(jnp.int32)


def draw_amp_tiles(key, part):
    return locality(key, NO // TILE, NV // TILE, 11)


def draw_int_tiles(key, part):
    return locality(key, NV // TILE, NA // TILE, 23)


def with_spikes(values, own_key, source, target, shards_of, factor):
    owner, partner = [(jnp.arange(values.shape[position]) // (values.shape[position] // shards_of)).reshape([-1 if axis == position else 1 for axis in range(values.ndim)]) for position in (source, target)]
    chosen = jax.random.permutation(own_key, shards_of)[partner]
    strong = (owner == chosen) | (owner == (partner + shards_of // 2) % shards_of)
    return jnp.where(strong, factor * values, values)


def level_of(key, extent, cuts, least, high):
    factor_of, own = 1.0, jax.random.fold_in(key, 6)
    for axis_at, shards_of in cuts:
        draws = jnp.exp(jax.random.uniform(jax.random.fold_in(own, axis_at), (shards_of,), jnp.float32, least / len(cuts), high / len(cuts)))
        factor_of = factor_of * jnp.repeat(draws, extent[axis_at] // shards_of).reshape([-1 if axis == axis_at else 1 for axis in range(len(extent))])
    return factor_of


def bell_draw(rng, shape, deviation, bound, shards=(), kind=jnp.bfloat16):
    factor_of = level_of(rng, shape, shards, -0.22, 0.18) if shards else 1.0
    entries = jax.random.normal(rng, shape, jnp.float32) * deviation * factor_of
    return jnp.minimum(jnp.maximum(entries, -bound), bound).astype(kind)


def noise_with(key, shape, scale, reach, pieces, heavy, held_as=jnp.bfloat16):
    entries = scale * jax.random.normal(key, shape, jnp.float32)
    if pieces:
        entries = entries * level_of(key, shape, pieces, -0.22, 0.18)
    return jnp.clip(with_spikes(entries, jax.random.fold_in(key, 3), *heavy), -reach, reach).astype(held_as)


def setup_inputs(seed: int = 0) -> dict:
    key_of = jax.random.split(jax.random.key(seed), 6)
    return {
        "amplitudes": bell_draw(key_of[0], (NO, NV), 1.0, 6.0, ((0, 4), (1, 8))),
        "amp_tiles": draw_amp_tiles(jax.random.fold_in(key_of[5], 71), 0),
        "occ_coupling": bell_draw(key_of[2], (OCC, OCC), OCC ** -0.5, 0.5),
        "integrals": noise_with(key_of[3], (NV, NA), NV ** -0.5, 0.09375, ((0, 8),), (0, 1, 8, 2.0)),
        "int_tiles": draw_int_tiles(jax.random.fold_in(key_of[5], 71), 0),
    }


def keep_tiles(values, tiles):
    height, width = values.shape
    blocks = values.reshape(height // TILE, TILE, width // TILE, TILE)
    kept = blocks * tiles.astype(values.dtype)[:, None, :, None]
    return kept.reshape(height, width)


def reference(amplitudes, amp_tiles, occ_coupling, integrals, int_tiles):
    amp_kept = keep_tiles(amplitudes, amp_tiles)
    int_kept = keep_tiles(integrals, int_tiles)
    pairs_v = amp_kept.shape[1]
    by_second = amp_kept.reshape(OCC, OCC, pairs_v).transpose(1, 0, 2)

    def dress_slab(slab):
        mixed = jnp.dot(occ_coupling, slab, preferred_element_type=jnp.float32)
        return (slab.astype(jnp.float32) + mixed).astype(jnp.bfloat16)

    dressed = lax.map(dress_slab, by_second).transpose(1, 0, 2).reshape(OCC * OCC, pairs_v)
    tau = keep_tiles(dressed, amp_tiles)
    tau_blocks = tau.reshape(OCC * OCC, N_CUTS, CD_DEV).transpose(1, 0, 2)
    int_blocks = int_kept.reshape(N_CUTS, CD_DEV, int_kept.shape[1])

    def add_block(total, pair):
        tau_b, int_b = pair
        part = lax.dot_general(int_b, tau_b, (((0,), (1,)), ((), ())), preferred_element_type=jnp.float32)
        part = lax.optimization_barrier(part.astype(jnp.bfloat16)).astype(jnp.float32)
        return total + part, None

    start = jnp.zeros((int_kept.shape[1], OCC * OCC), jnp.float32)
    total, unused = lax.scan(add_block, start, (tau_blocks, int_blocks))
    return total.astype(jnp.bfloat16)
```

```python
import functools

import jax
import jax.numpy as jnp
from jax import lax
from jax.experimental import pallas as pl
from jax.experimental.pallas import tpu as pltpu
from jax.sharding import PartitionSpec as P

TILE = 128
CHUNKS = 4


def keep_tiles(values, tiles):
    height, width = values.shape
    blocks = values.reshape(height // TILE, TILE, width // TILE, TILE)
    kept = blocks * tiles.astype(values.dtype)[:, None, :, None]
    return kept.reshape(height, width)


def ladder_kernel(rows_at, amp_ref, mask_ref, occ_ref, int_ref, out_ref):
    mask = mask_ref[...]
    occ = occ_ref[...]
    slabs = []
    for at in range(rows_at):
        pieces = [amp_ref[src, at] for src in range(amp_ref.shape[0])]
        slab = jnp.concatenate(pieces, axis=0) * mask
        mixed = jnp.dot(occ, slab, preferred_element_type=jnp.float32)
        dressed = (slab.astype(jnp.float32) + mixed).astype(jnp.bfloat16)
        slabs.append(dressed * mask)
    tau = jnp.concatenate(slabs, axis=0)
    width = out_ref.shape[2]
    for owner in range(out_ref.shape[0]):
        part = jnp.dot(
            tau, int_ref[:, owner * width : (owner + 1) * width], preferred_element_type=jnp.float32
        )
        out_ref[owner] = part.astype(jnp.bfloat16)


def ladder(arrived, mask, occ_coupling, int_kept, owners):
    sources, seconds, firsts, cols = arrived.shape
    occ_all = occ_coupling.shape[0]
    width = int_kept.shape[1] // owners
    rows_at = 2 if seconds % 2 == 0 else 1
    block = rows_at * occ_all
    rows = seconds * occ_all
    flops = 2 * rows * cols * (occ_all + owners * width)
    moved = 2 * (rows * cols + cols * owners * width + rows * owners * width)
    return pl.pallas_call(
        functools.partial(ladder_kernel, rows_at),
        grid=(seconds // rows_at,),
        in_specs=[
            pl.BlockSpec((sources, rows_at, firsts, cols), lambda g: (0, g, 0, 0)),
            pl.BlockSpec((occ_all, cols), lambda g: (0, 0)),
            pl.BlockSpec((occ_all, occ_all), lambda g: (0, 0)),
            pl.BlockSpec((cols, owners * width), lambda g: (0, 0)),
        ],
        out_specs=pl.BlockSpec((owners, block, width), lambda g: (0, g, 0)),
        out_shape=jax.ShapeDtypeStruct((owners, rows, width), jnp.bfloat16),
        compiler_params=pltpu.CompilerParams(vmem_limit_bytes=40 * 1024 * 1024),
        cost_estimate=pl.CostEstimate(flops=flops, bytes_accessed=moved, transcendentals=0),
        name="ladder",
    )(arrived, mask, occ_coupling, int_kept)


def shards(amplitudes, amp_tiles, occ_coupling, integrals, int_tiles):
    local_rows, local_cols = amplitudes.shape
    occ_all = occ_coupling.shape[0]
    first_dev = local_rows // occ_all
    peers = lax.axis_size("bulk")
    owners = lax.axis_size("cuts")
    second_dev = occ_all // peers
    step = second_dev // CHUNKS
    tiles_all = lax.all_gather(amp_tiles.astype(jnp.bfloat16), "bulk", axis=0, tiled=True)
    mask = jnp.repeat(tiles_all, TILE, axis=1)
    int_kept = keep_tiles(integrals, int_tiles)
    by_owner = amplitudes.reshape(first_dev, peers, CHUNKS, step, local_cols)
    finished = []
    for at in range(CHUNKS):
        sent = by_owner[:, :, at].transpose(1, 2, 0, 3)
        arrived = lax.all_to_all(sent, "bulk", split_axis=0, concat_axis=0, tiled=True)
        partial = ladder(arrived, mask, occ_coupling, int_kept, owners)
        total = lax.psum_scatter(partial, "cuts", scatter_dimension=0, tiled=False)
        width = total.shape[1]
        back = total.reshape(step, peers, first_dev, width)
        back = lax.all_to_all(back, "bulk", split_axis=1, concat_axis=1, tiled=True)
        finished.append(back)
    joined = jnp.stack(finished, axis=0)
    out = joined.transpose(4, 3, 2, 0, 1)
    return out.reshape(out.shape[0], local_rows)


def solution(mesh):
    in_specs = (P("bulk", "cuts"), P("bulk", "cuts"), P(), P("cuts", None), P("cuts", None))
    out_specs = P("cuts", "bulk")
    return jax.shard_map(shards, mesh=mesh, in_specs=in_specs, out_specs=out_specs, check_vma=False)
```

```python
import functools

import jax
import jax.numpy as jnp
from jax import lax
from jax.experimental import pallas as pl
from jax.experimental.pallas import tpu as pltpu
from jax.sharding import Mesh, PartitionSpec as P

TILE = 128
CORES = 2
GROUP = ("bulk", "core")


def keep_tiles(values, tiles):
    height, width = values.shape
    blocks = values.reshape(height // TILE, TILE, width // TILE, TILE)
    kept = blocks * tiles.astype(values.dtype)[:, None, :, None]
    return kept.reshape(height, width)


def ladder_kernel(rows_at, amp_ref, mask_ref, occ_ref, int_ref, out_ref):
    occ = occ_ref[...]
    peers, cores, _, firsts, cols = amp_ref.shape
    occ_all = occ.shape[0]
    slabs = []
    for at in range(rows_at):
        halves = []
        for core in range(cores):
            mask = mask_ref[:, core * cols : (core + 1) * cols]
            pieces = [amp_ref[src, core, at] for src in range(peers)]
            slab = jnp.concatenate(pieces, axis=0) * mask
            mixed = jnp.dot(occ, slab, preferred_element_type=jnp.float32)
            dressed = (slab.astype(jnp.float32) + mixed).astype(jnp.bfloat16)
            halves.append(dressed * mask)
        slabs.append(jnp.concatenate(halves, axis=1))
    tau = jnp.concatenate(slabs, axis=0)
    width = out_ref.shape[-1]
    for owner in range(out_ref.shape[0]):
        for core in range(cores):
            start = (owner * cores + core) * width
            part = jnp.dot(
                tau, int_ref[:, start : start + width], preferred_element_type=jnp.float32
            ).astype(jnp.bfloat16)
            for at in range(rows_at):
                for peer in range(peers):
                    row = at * occ_all + peer * firsts
                    out_ref[owner, peer, core, at] = part[row : row + firsts]


def ladder(arrived, mask, occ_coupling, int_kept, owners):
    peers, cores, seconds, firsts, cols = arrived.shape
    occ_all = occ_coupling.shape[0]
    depth, total = int_kept.shape
    width = total // (owners * cores)
    rows_at = 2 if seconds % 2 == 0 else 1
    rows = seconds * occ_all
    flops = 2 * rows * depth * (occ_all + total)
    moved = 2 * (rows * depth + depth * total + rows * total)
    return pl.pallas_call(
        functools.partial(ladder_kernel, rows_at),
        grid=(seconds // rows_at,),
        in_specs=[
            pl.BlockSpec((peers, cores, rows_at, firsts, cols), lambda g: (0, 0, g, 0, 0)),
            pl.BlockSpec((occ_all, depth), lambda g: (0, 0)),
            pl.BlockSpec((occ_all, occ_all), lambda g: (0, 0)),
            pl.BlockSpec((depth, total), lambda g: (0, 0), pipeline_mode=pl.Buffered(1)),
        ],
        out_specs=pl.BlockSpec(
            (owners, peers, cores, rows_at, firsts, width), lambda g: (0, 0, 0, g, 0, 0)
        ),
        out_shape=jax.ShapeDtypeStruct(
            (owners, peers, cores, seconds, firsts, width), jnp.bfloat16
        ),
        compiler_params=pltpu.CompilerParams(vmem_limit_bytes=48 * 1024 * 1024),
        cost_estimate=pl.CostEstimate(flops=flops, bytes_accessed=moved, transcendentals=0),
        name="ladder",
    )(arrived, mask, occ_coupling, int_kept)


def chunk_sizes(seconds):
    if seconds % 16 == 0:
        unit = seconds // 16
        return [2 * unit, 4 * unit, 4 * unit, 6 * unit]
    pieces = min(4, seconds)
    return [seconds // pieces] * (pieces - 1) + [seconds - seconds // pieces * (pieces - 1)]


def shards(amplitudes, amp_tiles, occ_coupling, integrals, int_tiles):
    local_rows, local_cols = amplitudes.shape
    occ_all = occ_coupling.shape[0]
    first_dev = local_rows // occ_all
    peers = lax.axis_size("bulk")
    cores = lax.axis_size("core")
    owners = lax.axis_size("z")
    second_dev = occ_all // (peers * cores)
    int_kept = lax.all_gather(keep_tiles(integrals, int_tiles), "core", axis=0, tiled=True)
    tiles_all = lax.all_gather(amp_tiles.astype(jnp.bfloat16), GROUP, axis=0, tiled=True)
    tiles_all = tiles_all.reshape(peers, cores, first_dev, local_cols // TILE)
    tiles_all = tiles_all.transpose(0, 2, 1, 3).reshape(occ_all, cores * (local_cols // TILE))
    mask = jnp.repeat(tiles_all, TILE, axis=1)
    by_owner = amplitudes.reshape(first_dev, peers * cores, second_dev, local_cols)
    finished = []
    begin = 0
    for step in chunk_sizes(second_dev):
        sent = by_owner[:, :, begin : begin + step].transpose(1, 2, 0, 3)
        begin += step
        arrived = lax.all_to_all(sent, GROUP, split_axis=0, concat_axis=0, tiled=True)
        arrived = arrived.reshape(peers, cores, step, first_dev, local_cols)
        partial = ladder(arrived, mask, occ_coupling, int_kept, owners)
        total = lax.psum_scatter(partial, "z", scatter_dimension=0, tiled=False)
        width = total.shape[-1]
        total = total.reshape(peers * cores, step, first_dev, width)
        back = lax.all_to_all(total, GROUP, split_axis=0, concat_axis=0, tiled=True)
        finished.append(back)
    joined = jnp.concatenate(finished, axis=1).reshape(occ_all, first_dev, width)
    return joined.transpose(2, 1, 0).reshape(width, local_rows)


def solution(mesh):
    bulk, cuts = mesh.devices.shape
    split = Mesh(mesh.devices.reshape(bulk, cuts // CORES, CORES), ("bulk", "z", "core"))
    along = ("z", "core")
    in_specs = (P("bulk", along), P("bulk", along), P(), P(along, None), P(along, None))
    out_specs = P(along, "bulk")
    return jax.shard_map(shards, mesh=split, in_specs=in_specs, out_specs=out_specs, check_vma=False)
```

```python
import functools

import jax
import jax.numpy as jnp
from jax import lax
from jax.experimental import pallas as pl
from jax.experimental.pallas import tpu as pltpu
from jax.sharding import Mesh, PartitionSpec as P

TILE = 128
CORES = 2
GROUP = ("bulk", "core")


def keep_tiles(values, tiles):
    height, width = values.shape
    blocks = values.reshape(height // TILE, TILE, width // TILE, TILE)
    kept = blocks * tiles.astype(values.dtype)[:, None, :, None]
    return kept.reshape(height, width)


def ladder_kernel(rows_at, amp_ref, mask_ref, occ_ref, int_ref, out_ref):
    occ = occ_ref[...]
    peers, cores, _, firsts, cols = amp_ref.shape
    occ_all = occ.shape[0]
    slabs = []
    for at in range(rows_at):
        halves = []
        for core in range(cores):
            mask = mask_ref[:, core * cols : (core + 1) * cols]
            pieces = [amp_ref[src, core, at] for src in range(peers)]
            slab = jnp.concatenate(pieces, axis=0) * mask
            mixed = jnp.dot(occ, slab, preferred_element_type=jnp.float32)
            dressed = (slab.astype(jnp.float32) + mixed).astype(jnp.bfloat16)
            halves.append(dressed * mask)
        slabs.append(jnp.concatenate(halves, axis=1))
    tau = jnp.concatenate(slabs, axis=0)
    width = out_ref.shape[-1]
    for owner in range(out_ref.shape[0]):
        for core in range(cores):
            start = (owner * cores + core) * width
            part = jnp.dot(
                tau, int_ref[:, start : start + width], preferred_element_type=jnp.float32
            ).astype(jnp.bfloat16)
            for at in range(rows_at):
                for peer in range(peers):
                    row = at * occ_all + peer * firsts
                    out_ref[owner, peer, core, at] = part[row : row + firsts]


def ladder(arrived, mask, occ_coupling, int_kept, owners):
    peers, cores, seconds, firsts, cols = arrived.shape
    occ_all = occ_coupling.shape[0]
    depth, total = int_kept.shape
    width = total // (owners * cores)
    rows_at = 2 if seconds % 2 == 0 else 1
    rows = seconds * occ_all
    flops = 2 * rows * depth * (occ_all + total)
    moved = 2 * (rows * depth + depth * total + rows * total)
    return pl.pallas_call(
        functools.partial(ladder_kernel, rows_at),
        grid=(seconds // rows_at,),
        in_specs=[
            pl.BlockSpec((peers, cores, rows_at, firsts, cols), lambda g: (0, 0, g, 0, 0)),
            pl.BlockSpec((occ_all, depth), lambda g: (0, 0)),
            pl.BlockSpec((occ_all, occ_all), lambda g: (0, 0)),
            pl.BlockSpec((depth, total), lambda g: (0, 0), pipeline_mode=pl.Buffered(1)),
        ],
        out_specs=pl.BlockSpec(
            (owners, peers, cores, rows_at, firsts, width), lambda g: (0, 0, 0, g, 0, 0)
        ),
        out_shape=jax.ShapeDtypeStruct(
            (owners, peers, cores, seconds, firsts, width), jnp.bfloat16
        ),
        compiler_params=pltpu.CompilerParams(vmem_limit_bytes=48 * 1024 * 1024),
        cost_estimate=pl.CostEstimate(flops=flops, bytes_accessed=moved, transcendentals=0),
        name="ladder",
    )(arrived, mask, occ_coupling, int_kept)


def chunk_sizes(seconds):
    if seconds % 8 == 0:
        unit = seconds // 8
        return [2 * unit, 3 * unit, 3 * unit]
    pieces = min(3, seconds)
    first = seconds // pieces
    return [first] * (pieces - 1) + [seconds - first * (pieces - 1)]


def shards(amplitudes, amp_tiles, occ_coupling, integrals, int_tiles):
    local_rows, local_cols = amplitudes.shape
    occ_all = occ_coupling.shape[0]
    first_dev = local_rows // occ_all
    peers = lax.axis_size("bulk")
    cores = lax.axis_size("core")
    owners = lax.axis_size("z")
    group = peers * cores
    second_dev = occ_all // group
    swap = functools.partial(
        lax.all_to_all, axis_name=GROUP, split_axis=0, concat_axis=0, tiled=True
    )
    by_owner = amplitudes.reshape(first_dev, group, second_dev, local_cols)
    sizes = chunk_sizes(second_dev)
    sent = []
    begin = 0
    for step in sizes:
        sent.append(by_owner[:, :, begin : begin + step].transpose(1, 2, 0, 3))
        begin += step
    tiles = amp_tiles.astype(jnp.bfloat16)
    tiles_all = swap(jnp.broadcast_to(tiles[None], (group,) + tiles.shape))
    tiles_all, first = lax.optimization_barrier((tiles_all, sent[0]))
    arrived = swap(first)
    int_kept = lax.all_gather(keep_tiles(integrals, int_tiles), "core", axis=0, tiled=True)
    tiles_all = tiles_all.reshape(peers, cores, first_dev, local_cols // TILE)
    tiles_all = tiles_all.transpose(0, 2, 1, 3).reshape(occ_all, cores * (local_cols // TILE))
    mask = jnp.repeat(tiles_all, TILE, axis=1)
    finished = []
    for at, step in enumerate(sizes):
        if at + 1 < len(sizes):
            arrived, ready = lax.optimization_barrier((arrived, sent[at + 1]))
            following = swap(ready)
        arrived = arrived.reshape(peers, cores, step, first_dev, local_cols)
        partial = ladder(arrived, mask, occ_coupling, int_kept, owners)
        total = lax.psum_scatter(partial, "z", scatter_dimension=0, tiled=False)
        width = total.shape[-1]
        finished.append(swap(total.reshape(group, step, first_dev, width)))
        arrived = following
    joined = jnp.concatenate(finished, axis=1).reshape(occ_all, first_dev, width)
    return joined.transpose(2, 1, 0).reshape(width, local_rows)


def solution(mesh):
    bulk, cuts = mesh.devices.shape
    split = Mesh(mesh.devices.reshape(bulk, cuts // CORES, CORES), ("bulk", "z", "core"))
    along = ("z", "core")
    in_specs = (P("bulk", along), P("bulk", along), P(), P(along, None), P(along, None))
    out_specs = P(along, "bulk")
    return jax.shard_map(shards, mesh=split, in_specs=in_specs, out_specs=out_specs, check_vma=False)
```

```python
import functools

import jax
import jax.numpy as jnp
from jax import lax
from jax.experimental import pallas as pl
from jax.experimental.pallas import tpu as pltpu
from jax.sharding import Mesh, PartitionSpec as P

TILE = 128
CORES = 2
GROUP = ("bulk", "core")


def keep_tiles(values, tiles):
    height, width = values.shape
    blocks = values.reshape(height // TILE, TILE, width // TILE, TILE)
    kept = blocks * tiles.astype(values.dtype)[:, None, :, None]
    return kept.reshape(height, width)


def ladder_kernel(rows_at, amp_ref, mask_ref, occ_ref, int_ref, out_ref):
    occ = occ_ref[...]
    peers, cores, _, firsts, cols = amp_ref.shape
    occ_all = occ.shape[0]
    slabs = []
    for at in range(rows_at):
        halves = []
        for core in range(cores):
            mask = jnp.concatenate([mask_ref[src, core] for src in range(peers)], axis=0)
            pieces = [amp_ref[src, core, at] for src in range(peers)]
            slab = jnp.concatenate(pieces, axis=0) * mask
            mixed = jnp.dot(occ, slab, preferred_element_type=jnp.float32)
            dressed = (slab.astype(jnp.float32) + mixed).astype(jnp.bfloat16)
            halves.append(dressed * mask)
        slabs.append(jnp.concatenate(halves, axis=1))
    tau = jnp.concatenate(slabs, axis=0)
    width = out_ref.shape[-1]
    for owner in range(out_ref.shape[0]):
        for core in range(cores):
            start = (owner * cores + core) * width
            part = jnp.dot(
                tau, int_ref[:, start : start + width], preferred_element_type=jnp.float32
            ).astype(jnp.bfloat16)
            for at in range(rows_at):
                for peer in range(peers):
                    row = at * occ_all + peer * firsts
                    out_ref[owner, peer, core, at] = part[row : row + firsts]


def ladder(arrived, mask, occ_coupling, int_kept, owners):
    peers, cores, seconds, firsts, cols = arrived.shape
    occ_all = occ_coupling.shape[0]
    depth, total = int_kept.shape
    width = total // (owners * cores)
    rows_at = 2 if seconds % 2 == 0 else 1
    rows = seconds * occ_all
    flops = 2 * rows * depth * (occ_all + total)
    moved = 2 * (rows * depth + depth * total + rows * total)
    return pl.pallas_call(
        functools.partial(ladder_kernel, rows_at),
        grid=(seconds // rows_at,),
        in_specs=[
            pl.BlockSpec((peers, cores, rows_at, firsts, cols), lambda g: (0, 0, g, 0, 0)),
            pl.BlockSpec((peers, cores, firsts, cols), lambda g: (0, 0, 0, 0)),
            pl.BlockSpec((occ_all, occ_all), lambda g: (0, 0)),
            pl.BlockSpec((depth, total), lambda g: (0, 0), pipeline_mode=pl.Buffered(1)),
        ],
        out_specs=pl.BlockSpec(
            (owners, peers, cores, rows_at, firsts, width), lambda g: (0, 0, 0, g, 0, 0)
        ),
        out_shape=jax.ShapeDtypeStruct(
            (owners, peers, cores, seconds, firsts, width), jnp.bfloat16
        ),
        compiler_params=pltpu.CompilerParams(vmem_limit_bytes=48 * 1024 * 1024),
        cost_estimate=pl.CostEstimate(flops=flops, bytes_accessed=moved, transcendentals=0),
        name="ladder",
    )(arrived, mask, occ_coupling, int_kept)


def chunk_sizes(seconds):
    if seconds % 8 == 0:
        unit = seconds // 8
        return [2 * unit, 3 * unit, 3 * unit]
    pieces = min(3, seconds)
    first = seconds // pieces
    return [first] * (pieces - 1) + [seconds - first * (pieces - 1)]


def gather_maps(spread, peers, cores):
    swapped = lax.ppermute(spread, "core", [(at, 1 - at) for at in range(cores)])
    first = lax.axis_index("core") == 0
    pair = jnp.stack([jnp.where(first, spread, swapped), jnp.where(first, swapped, spread)])
    shifts = [pair] + [
        lax.ppermute(pair, "bulk", [(at, (at + shift) % peers) for at in range(peers)])
        for shift in range(1, peers)
    ]
    doubled = jnp.stack(shifts[::-1] + shifts[::-1])
    start = lax.rem(2 * peers - 1 - lax.axis_index("bulk"), peers)
    return lax.dynamic_slice_in_dim(doubled, start, peers, axis=0)


def shards(amplitudes, amp_tiles, occ_coupling, integrals, int_tiles):
    local_rows, local_cols = amplitudes.shape
    occ_all = occ_coupling.shape[0]
    first_dev = local_rows // occ_all
    peers = lax.axis_size("bulk")
    cores = lax.axis_size("core")
    owners = lax.axis_size("z")
    group = peers * cores
    second_dev = occ_all // group
    swap = functools.partial(
        lax.all_to_all, axis_name=GROUP, split_axis=0, concat_axis=0, tiled=True
    )
    by_owner = amplitudes.reshape(first_dev, group, second_dev, local_cols)
    sizes = chunk_sizes(second_dev)
    sent = []
    begin = 0
    for step in sizes:
        sent.append(by_owner[:, :, begin : begin + step].transpose(1, 2, 0, 3))
        begin += step
    arrived = swap(sent[0])
    int_kept = lax.all_gather(keep_tiles(integrals, int_tiles), "core", axis=0, tiled=True)
    mask = gather_maps(jnp.repeat(amp_tiles.astype(jnp.bfloat16), TILE, axis=1), peers, cores)
    finished = []
    for at, step in enumerate(sizes):
        if at + 1 < len(sizes):
            arrived, ready = lax.optimization_barrier((arrived, sent[at + 1]))
            following = swap(ready)
        arrived = arrived.reshape(peers, cores, step, first_dev, local_cols)
        partial = ladder(arrived, mask, occ_coupling, int_kept, owners)
        total = lax.psum_scatter(partial, "z", scatter_dimension=0, tiled=False)
        width = total.shape[-1]
        finished.append(swap(total.reshape(group, step, first_dev, width)))
        arrived = following
    joined = jnp.concatenate(finished, axis=1).reshape(occ_all, first_dev, width)
    return joined.transpose(2, 1, 0).reshape(width, local_rows)


def solution(mesh):
    bulk, cuts = mesh.devices.shape
    split = Mesh(mesh.devices.reshape(bulk, cuts // CORES, CORES), ("bulk", "z", "core"))
    along = ("z", "core")
    in_specs = (P("bulk", along), P("bulk", along), P(), P(along, None), P(along, None))
    out_specs = P(along, "bulk")
    return jax.shard_map(shards, mesh=split, in_specs=in_specs, out_specs=out_specs, check_vma=False)
```

```python
import functools

import jax
import jax.numpy as jnp
from jax import lax
from jax.experimental import pallas as pl
from jax.experimental.pallas import tpu as pltpu
from jax.sharding import Mesh, PartitionSpec as P

TILE = 128
CORES = 2
GROUP = ("bulk", "core")


def keep_tiles(values, tiles):
    height, width = values.shape
    blocks = values.reshape(height // TILE, TILE, width // TILE, TILE)
    kept = blocks * tiles.astype(values.dtype)[:, None, :, None]
    return kept.reshape(height, width)


def ladder_kernel(rows_at, amp_ref, mask_ref, occ_ref, int_ref, out_ref):
    occ = occ_ref[...]
    peers, cores, _, firsts, cols = amp_ref.shape
    occ_all = occ.shape[0]
    slabs = []
    for at in range(rows_at):
        halves = []
        for core in range(cores):
            mask = jnp.concatenate([mask_ref[src, core] for src in range(peers)], axis=0)
            pieces = [amp_ref[src, core, at] for src in range(peers)]
            slab = jnp.concatenate(pieces, axis=0) * mask
            mixed = jnp.dot(occ, slab, preferred_element_type=jnp.float32)
            dressed = (slab.astype(jnp.float32) + mixed).astype(jnp.bfloat16)
            halves.append(dressed * mask)
        slabs.append(jnp.concatenate(halves, axis=1))
    tau = jnp.concatenate(slabs, axis=0)
    width = out_ref.shape[-1]
    for owner in range(out_ref.shape[0]):
        for core in range(cores):
            start = (owner * cores + core) * width
            part = jnp.dot(
                tau, int_ref[:, start : start + width], preferred_element_type=jnp.float32
            ).astype(jnp.bfloat16)
            for at in range(rows_at):
                for peer in range(peers):
                    row = at * occ_all + peer * firsts
                    out_ref[owner, peer, core, at] = part[row : row + firsts]


def ladder(arrived, mask, occ_coupling, int_kept, owners):
    peers, cores, seconds, firsts, cols = arrived.shape
    occ_all = occ_coupling.shape[0]
    depth, total = int_kept.shape
    width = total // (owners * cores)
    rows_at = 2 if seconds % 2 == 0 else 1
    rows = seconds * occ_all
    flops = 2 * rows * depth * (occ_all + total)
    moved = 2 * (rows * depth + depth * total + rows * total)
    return pl.pallas_call(
        functools.partial(ladder_kernel, rows_at),
        grid=(seconds // rows_at,),
        in_specs=[
            pl.BlockSpec((peers, cores, rows_at, firsts, cols), lambda g: (0, 0, g, 0, 0)),
            pl.BlockSpec((peers, cores, firsts, cols), lambda g: (0, 0, 0, 0)),
            pl.BlockSpec((occ_all, occ_all), lambda g: (0, 0)),
            pl.BlockSpec((depth, total), lambda g: (0, 0), pipeline_mode=pl.Buffered(1)),
        ],
        out_specs=pl.BlockSpec(
            (owners, peers, cores, rows_at, firsts, width), lambda g: (0, 0, 0, g, 0, 0)
        ),
        out_shape=jax.ShapeDtypeStruct(
            (owners, peers, cores, seconds, firsts, width), jnp.bfloat16
        ),
        compiler_params=pltpu.CompilerParams(vmem_limit_bytes=48 * 1024 * 1024),
        cost_estimate=pl.CostEstimate(flops=flops, bytes_accessed=moved, transcendentals=0),
        name="ladder",
    )(arrived, mask, occ_coupling, int_kept)


def chunk_sizes(seconds):
    if seconds % 8 == 0:
        unit = seconds // 8
        return [2 * unit, 3 * unit, 3 * unit]
    pieces = min(3, seconds)
    first = seconds // pieces
    return [first] * (pieces - 1) + [seconds - first * (pieces - 1)]


def gather_maps(spread, peers, cores):
    swapped = lax.ppermute(spread, "core", [(at, 1 - at) for at in range(cores)])
    first = lax.axis_index("core") == 0
    pair = jnp.stack([jnp.where(first, spread, swapped), jnp.where(first, swapped, spread)])
    shifts = [pair] + [
        lax.ppermute(pair, "bulk", [(at, (at + shift) % peers) for at in range(peers)])
        for shift in range(1, peers)
    ]
    doubled = jnp.stack(shifts[::-1] + shifts[::-1])
    start = lax.rem(2 * peers - 1 - lax.axis_index("bulk"), peers)
    return lax.dynamic_slice_in_dim(doubled, start, peers, axis=0)


def shards(amplitudes, amp_tiles, occ_coupling, integrals, int_tiles):
    local_rows, local_cols = amplitudes.shape
    occ_all = occ_coupling.shape[0]
    first_dev = local_rows // occ_all
    peers = lax.axis_size("bulk")
    cores = lax.axis_size("core")
    owners = lax.axis_size("z")
    group = peers * cores
    second_dev = occ_all // group
    swap = functools.partial(
        lax.all_to_all, axis_name=GROUP, split_axis=0, concat_axis=0, tiled=True
    )
    by_owner = amplitudes.reshape(first_dev, group, second_dev, local_cols)
    sizes = chunk_sizes(second_dev)
    sent = []
    begin = 0
    for step in sizes:
        sent.append(by_owner[:, :, begin : begin + step].transpose(1, 2, 0, 3))
        begin += step
    arrived = swap(sent[0])
    int_kept = lax.all_gather(keep_tiles(integrals, int_tiles), "core", axis=0, tiled=True)
    mask = gather_maps(jnp.repeat(amp_tiles.astype(jnp.bfloat16), TILE, axis=1), peers, cores)
    finished = []
    for at, step in enumerate(sizes):
        ahead = at + 1 < len(sizes)
        if at == 0 and ahead:
            arrived, *sent[1:] = lax.optimization_barrier((arrived, *sent[1:]))
            following = swap(sent[1])
        arrived = arrived.reshape(peers, cores, step, first_dev, local_cols)
        partial = ladder(arrived, mask, occ_coupling, int_kept, owners)
        if at > 0 and ahead:
            partial, ready = lax.optimization_barrier((partial, sent[at + 1]))
            following = swap(ready)
        total = lax.psum_scatter(partial, "z", scatter_dimension=0, tiled=False)
        width = total.shape[-1]
        finished.append(swap(total.reshape(group, step, first_dev, width)))
        arrived = following
    joined = jnp.concatenate(finished, axis=1).reshape(occ_all, first_dev, width)
    return joined.transpose(2, 1, 0).reshape(width, local_rows)


def solution(mesh):
    bulk, cuts = mesh.devices.shape
    split = Mesh(mesh.devices.reshape(bulk, cuts // CORES, CORES), ("bulk", "z", "core"))
    along = ("z", "core")
    in_specs = (P("bulk", along), P("bulk", along), P(), P(along, None), P(along, None))
    out_specs = P(along, "bulk")
    return jax.shard_map(shards, mesh=split, in_specs=in_specs, out_specs=out_specs, check_vma=False)
```
